32 devices in a mesh: dp: 8 (over z, x), tensor: 4 (over y, core).
Axes of the slice: x: 2, y: 2, z: 4, core: 2. Of those that a mesh axis runs over, the one named last changes fastest.
Arguments:
- block_input: bfloat16 [4608, 1024], P(('dp', 'tensor')), may hold values from -6 to 6
- cotangent: bfloat16 [4608, 1024], P(('dp', 'tensor')), may hold values from -6 to 6
- norm_gains: float32 [2, 1024], P(None, ('dp', 'tensor')), may hold values from 0.5 to 1.5
- norm_shifts: float32 [3, 1024], P(None, ('dp', 'tensor')), may hold values from -1.8 to 1.8
- qkv_weight: bfloat16 [1024, 3072], P('dp', 'tensor'), may hold values from -0.1875 to 0.1875
- qkv_bias: bfloat16 [48, 64], P('tensor', 'dp'), may hold values from -3 to 3
- out_weight: bfloat16 [1024, 1024], P('tensor', 'dp'), may hold values from -0.75 to 0.75
- up_weight: bfloat16 [1024, 4096], P('dp', 'tensor'), may hold values from -0.1875 to 0.1875
- up_bias: bfloat16 [64, 64], P('tensor', 'dp'), may hold values from -3 to 3
- down_weight: bfloat16 [4096, 1024], P('tensor', 'dp'), may hold values from -0.09375 to 0.09375
Outputs:
- output: bfloat16 [4608, 1024], P(('dp', 'tensor'))
- input_grad: bfloat16 [4608, 1024], P(('dp', 'tensor'))
- grad_norm_gains: float32 [2, 1024], P(None, ('dp', 'tensor'))
- grad_norm_shifts: float32 [3, 1024], P(None, ('dp', 'tensor'))
- grad_qkv_weight: float32 [1024, 3072], P('dp', 'tensor')
- grad_qkv_bias: float32 [48, 64], P('tensor', 'dp')
- grad_out_weight: float32 [1024, 1024], P('tensor', 'dp')
- grad_up_weight: float32 [1024, 4096], P('dp', 'tensor')
- grad_up_bias: float32 [64, 64], P('tensor', 'dp')
- grad_down_weight: float32 [4096, 1024], P('tensor', 'dp')
The draws below stay inside these ranges and needn't reach their ends.
All inputs are finite; a program needn't handle non-finite values.
Results may differ from the reference program's by a relative error of at most 0.013.
Values may be sent and summed in bfloat16 or wider, within the bound.
No kernel may reach another device: no remote copies, remote signals or barrier semaphores. Data moves between devices by JAX's collectives and lax.ppermute only.
A program may use at most 128 MiB of HBM per device.

```python
import jax
import jax.numpy as jnp
from jax import lax

D = 1024
HEADS = 16
HEAD = 64
FF = 4096
ROT = 16
LEN = 576
TOKENS = 4608


def raised(result, rng, source, target, parts, factor):
    def block_of(dim):
        return (jnp.arange(result.shape[dim]) // (result.shape[dim] // parts)).reshape((-1,) + (1,) * (result.ndim - 1 - dim))

    first = jax.random.permutation(rng, parts)[block_of(target)]
    other_side = (block_of(target) + parts // 2) % parts
    return jnp.where((block_of(source) == first) | (block_of(source) == other_side), factor * result, result)


def block_scale(own_key, extent, shards, low, top_value):
    def one(axis_at, shards_of):
        heights = jax.random.uniform(jax.random.fold_in(jax.random.fold_in(own_key, 6), axis_at), (shards_of,), jnp.float32, low / len(shards), top_value / len(shards))
        return jnp.repeat(jnp.exp(heights), extent[axis_at] // shards_of).reshape((-1,) + (1,) * (len(extent) - axis_at - 1))

    factor_of = one(*shards[0])
    for cut in shards[1:]:
        factor_of = factor_of * one(*cut)
    return factor_of


def bell_draw(key, shape, scale, bound, cuts=(), kind=jnp.bfloat16):
    gain = block_scale(key, shape, cuts, -0.22, 0.18) if cuts else 1.0
    array = jax.random.normal(key, shape, jnp.float32) * scale * gain
    return jnp.minimum(jnp.maximum(array, -bound), bound).astype(kind)


def gaussian_with(own_key, shape, width, reach, shards, heavy, held_as=jnp.bfloat16):
    values = width * jax.random.normal(own_key, shape, jnp.float32)
    if shards:
        values = values * block_scale(own_key, shape, shards, -0.22, 0.18)
    return jnp.clip(raised(values, jax.random.fold_in(own_key, 3), *heavy), -reach, reach).astype(held_as)


def setup_inputs(seed: int = 0) -> dict:
    seeds = jax.random.split(jax.random.key(seed), 11)
    return {
        "block_input": bell_draw(seeds[0], (TOKENS, D), 1.0, 6.0, ((0, 32),)),
        "cotangent": gaussian_with(seeds[1], (TOKENS, D), 1.0, 6.0, ((0, 32),), (0, 1, 32, 2.75)),
        "norm_gains": jnp.clip(1.0 + 0.1 * jax.random.normal(seeds[2], (2, D), jnp.float32), 0.5, 1.5),
        "norm_shifts": bell_draw(seeds[3], (3, D), 0.3, 1.8, ((1, 32),), jnp.float32),
        "qkv_weight": bell_draw(seeds[4], (D, 3 * D), D ** -0.5, 0.1875, ((0, 8), (1, 4))),
        "qkv_bias": bell_draw(seeds[5], (3 * HEADS, HEAD), 0.5, 3.0, ((0, 4), (1, 8))),
        "out_weight": bell_draw(seeds[6], (D, D), (D // 16) ** -0.5, 0.75, ((0, 4), (1, 8))),
        "up_weight": bell_draw(seeds[7], (D, FF), D ** -0.5, 0.1875, ((0, 8), (1, 4))),
        "up_bias": bell_draw(seeds[8], (FF // 64, 64), 0.5, 3.0, ((0, 4), (1, 8))),
        "down_weight": bell_draw(seeds[9], (FF, D), FF ** -0.5, 0.09375, ((0, 4), (1, 8))),
    }


EPSILON = 1e-05
SCALE = 0.125

def layer_norm(features, gain_row, shift_row):
    row_mean = lax.optimization_barrier(jnp.mean(features, axis=-1, keepdims=True))
    centred = features - row_mean
    row_var = lax.optimization_barrier(jnp.mean(centred * centred, axis=-1, keepdims=True))
    inv_scale = lax.rsqrt(row_var + EPSILON)
    unit_rows = centred * inv_scale
    return (unit_rows * gain_row + shift_row, unit_rows, inv_scale)

def norm_back(grad_rows, unit_rows, inv_scale, gain_row):
    scaled_grad = grad_rows * gain_row
    first_mean = lax.optimization_barrier(jnp.mean(scaled_grad, axis=-1, keepdims=True))
    second_mean = lax.optimization_barrier(jnp.mean(scaled_grad * unit_rows, axis=-1, keepdims=True))
    return inv_scale * (scaled_grad - first_mean - unit_rows * second_mean)

def gelu_slope(pre_act):
    return 0.5 * (1.0 + lax.erf(pre_act * 0.7071067811865476)) + pre_act * jnp.exp(-0.5 * pre_act * pre_act) * 0.3989422804014327

def rotary_tables():
    half_rot = ROT // 2
    position = jnp.arange(LEN, dtype=jnp.float32)[:, None]
    frequency = 10000.0 ** (-2.0 * jnp.arange(half_rot, dtype=jnp.float32) / ROT)
    angles = position * frequency[None, :]
    return (jnp.cos(angles)[:, None, :], jnp.sin(angles)[:, None, :])

def rotate(tensor, cos_table, sin_table):
    half_rot = ROT // 2
    front_half = tensor[..., :half_rot]
    back_half = tensor[..., half_rot:ROT]
    return jnp.concatenate([front_half * cos_table - back_half * sin_table, back_half * cos_table + front_half * sin_table, tensor[..., ROT:]], axis=-1)

def causal(length):
    row_ids = lax.broadcasted_iota(jnp.int32, (length, length), 0)
    col_ids = lax.broadcasted_iota(jnp.int32, (length, length), 1)
    return row_ids >= col_ids

def attend(queries, key_heads, values, allowed):
    scores = jnp.einsum('qhe,khe->hqk', queries.astype(jnp.float32), key_heads.astype(jnp.float32)) * SCALE
    masked = jnp.where(allowed, scores, -1e+30)
    row_top = lax.optimization_barrier(jnp.max(masked, axis=-1, keepdims=True))
    row_total = lax.optimization_barrier(jnp.sum(jnp.exp(masked - row_top), axis=-1, keepdims=True))
    log_sum = row_top + jnp.log(row_total)
    attn_probs = jnp.where(allowed, jnp.exp(masked - log_sum), 0.0).astype(jnp.bfloat16)
    context = jnp.einsum('hqk,khe->qhe', attn_probs.astype(jnp.float32), values.astype(jnp.float32))
    return (context.astype(jnp.bfloat16), log_sum)

def attend_back(queries, key_heads, values, log_sum, grad_context, allowed):
    scores = jnp.einsum('qhe,khe->hqk', queries.astype(jnp.float32), key_heads.astype(jnp.float32)) * SCALE
    masked = jnp.where(allowed, scores, -1e+30)
    exact = jnp.where(allowed, jnp.exp(masked - log_sum), 0.0)
    rounded = exact.astype(jnp.bfloat16)
    grad_value = jnp.einsum('hqk,qhe->khe', rounded.astype(jnp.float32), grad_context.astype(jnp.float32))
    grad_probs = jnp.einsum('qhe,khe->hqk', grad_context.astype(jnp.float32), values.astype(jnp.float32))
    row_dot = lax.optimization_barrier(jnp.sum(exact * grad_probs, axis=-1, keepdims=True))
    grad_scores = (exact * (grad_probs - row_dot) * SCALE).astype(jnp.bfloat16)
    grad_query = jnp.einsum('hqk,khe->qhe', grad_scores.astype(jnp.float32), key_heads.astype(jnp.float32))
    grad_key = jnp.einsum('hqk,qhe->khe', grad_scores.astype(jnp.float32), queries.astype(jnp.float32))
    return (grad_query, grad_key, grad_value)

def reference(block_input, cotangent, norm_gains, norm_shifts, qkv_weight, qkv_bias, out_weight, up_weight, up_bias, down_weight):
    cos_table, sin_table = rotary_tables()
    allowed = causal(LEN)
    qkv_flat = qkv_bias.reshape(-1).astype(jnp.float32)
    up_flat = up_bias.reshape(-1).astype(jnp.float32)

    def per_sequence(carry, member):
        inputs_seq, cot_seq = member
        residual = inputs_seq.astype(jnp.float32)
        cot_rows = cot_seq.astype(jnp.float32)
        normed_one, unit_one, inv_one = layer_norm(residual, norm_gains[0], norm_shifts[0])
        normed_two, unit_two, inv_two = layer_norm(residual, norm_gains[1], norm_shifts[1])
        normed_attn = normed_one.astype(jnp.bfloat16)
        normed_mlp = normed_two.astype(jnp.bfloat16)
        projected = (jnp.dot(normed_attn, qkv_weight, preferred_element_type=jnp.float32) + qkv_flat).reshape(LEN, HEADS, 3, HEAD)
        queries = rotate(projected[:, :, 0], cos_table, sin_table).astype(jnp.bfloat16)
        key_heads = rotate(projected[:, :, 1], cos_table, sin_table).astype(jnp.bfloat16)
        values = projected[:, :, 2].astype(jnp.bfloat16)
        context, log_sum = attend(queries, key_heads, values, allowed)
        context_rows = context.reshape(LEN, D)
        pre_act = jnp.dot(normed_mlp, up_weight, preferred_element_type=jnp.float32) + up_flat
        activation = jax.nn.gelu(pre_act, approximate=False).astype(jnp.bfloat16)
        branches = jnp.dot(context_rows, out_weight, preferred_element_type=jnp.float32) + jnp.dot(activation, down_weight, preferred_element_type=jnp.float32)
        output = (residual + branches + norm_shifts[2]).astype(jnp.bfloat16)
        grad_act = jnp.dot(cot_seq, down_weight.T, preferred_element_type=jnp.float32)
        grad_pre = (grad_act * gelu_slope(pre_act)).astype(jnp.bfloat16)
        grad_context = jnp.dot(cot_seq, out_weight.T, preferred_element_type=jnp.float32).astype(jnp.bfloat16).reshape(LEN, HEADS, HEAD)
        grad_query, grad_key, grad_value = attend_back(queries, key_heads, values, log_sum, grad_context, allowed)
        grad_query = rotate(grad_query, cos_table, -sin_table)
        grad_key = rotate(grad_key, cos_table, -sin_table)
        grad_qkv = jnp.stack([grad_query, grad_key, grad_value], axis=2).reshape(LEN, 3 * D).astype(jnp.bfloat16)
        grad_normed_attn = jnp.dot(grad_qkv, qkv_weight.T, preferred_element_type=jnp.float32)
        grad_normed_mlp = jnp.dot(grad_pre, up_weight.T, preferred_element_type=jnp.float32)
        input_grad = (cot_rows + norm_back(grad_normed_attn, unit_one, inv_one, norm_gains[0]) + norm_back(grad_normed_mlp, unit_two, inv_two, norm_gains[1])).astype(jnp.bfloat16)
        updates = (jnp.dot(normed_attn.T, grad_qkv, preferred_element_type=jnp.float32), jnp.dot(context_rows.T, cot_seq, preferred_element_type=jnp.float32), jnp.dot(normed_mlp.T, grad_pre, preferred_element_type=jnp.float32), jnp.dot(activation.T, cot_seq, preferred_element_type=jnp.float32), lax.optimization_barrier(jnp.sum(grad_qkv.astype(jnp.float32), axis=0)), lax.optimization_barrier(jnp.sum(grad_pre.astype(jnp.float32), axis=0)), jnp.stack([lax.optimization_barrier(jnp.sum(grad_normed_attn * unit_one, axis=0)), lax.optimization_barrier(jnp.sum(grad_normed_mlp * unit_two, axis=0))]), jnp.stack([lax.optimization_barrier(jnp.sum(grad_normed_attn, axis=0)), lax.optimization_barrier(jnp.sum(grad_normed_mlp, axis=0)), lax.optimization_barrier(jnp.sum(cot_rows, axis=0))]))
        return (jax.tree.map(jnp.add, carry, updates), (output, input_grad))
    start = (jnp.zeros((D, 3 * D), jnp.float32), jnp.zeros((D, D), jnp.float32), jnp.zeros((D, FF), jnp.float32), jnp.zeros((FF, D), jnp.float32), jnp.zeros((3 * D,), jnp.float32), jnp.zeros((FF,), jnp.float32), jnp.zeros((2, D), jnp.float32), jnp.zeros((3, D), jnp.float32))
    sequences = block_input.shape[0] // LEN
    totals, (outputs, grads_in) = lax.scan(per_sequence, start, (block_input.reshape(sequences, LEN, D), cotangent.reshape(sequences, LEN, D)))
    grad_qkv_weight, grad_out_weight, grad_up_weight, grad_down_weight, grad_qkv_flat, grad_up_flat, grad_norm_gains, grad_norm_shifts = totals
    return (outputs.reshape(-1, D), grads_in.reshape(-1, D), grad_norm_gains, grad_norm_shifts, grad_qkv_weight, grad_qkv_flat.reshape(3 * HEADS, HEAD), grad_out_weight, grad_up_weight, grad_up_flat.reshape(FF // 64, 64), grad_down_weight)
```

```python
import jax
import jax.numpy as jnp
from jax import lax
from jax.experimental import pallas as pl
from jax.experimental.pallas import tpu as pltpu
from jax.sharding import PartitionSpec as P

HEAD = 64
ROT = 16
LEN = 576
QB = 192

EPSILON = 1e-05
SCALE = 0.125

BF = jnp.bfloat16
F32 = jnp.float32


def dot(a, b, dims=((1,), (0,))):
    return lax.dot_general(a, b, (dims, ((), ())), preferred_element_type=F32)


def gelu_slope(pre_act):
    return (
        0.5 * (1.0 + lax.erf(pre_act * 0.7071067811865476))
        + pre_act * jnp.exp(-0.5 * pre_act * pre_act) * 0.3989422804014327
    )


def rotary_tables(width):
    half = ROT // 2
    lane = jnp.arange(width, dtype=jnp.int32)
    inside = lane % HEAD
    rotated = (inside < ROT) & (lane % (3 * HEAD) < 2 * HEAD)
    index = (inside % half).astype(F32)
    frequency = 10000.0 ** (-2.0 * index / ROT)
    angles = jnp.arange(LEN, dtype=F32)[:, None] * frequency[None, :]
    cosine, sine = jnp.cos(angles), jnp.sin(angles)
    low = rotated & (inside < half)
    high = rotated & (inside >= half)
    return (
        jnp.where(rotated[None], cosine, 1.0),
        jnp.where(low[None], -sine, 0.0),
        jnp.where(high[None], sine, 0.0),
    )


def attention_kernel(qkv_ref, gc_ref, cos_ref, low_ref, high_ref, ctx_ref, out_ref, dk_ref, dv_ref):
    half = ROT // 2
    width = qkv_ref.shape[1]
    raw = qkv_ref[...]
    cosine, low, high = cos_ref[...], low_ref[...], high_ref[...]
    turned = (
        raw * cosine
        + pltpu.roll(raw, width - half, 1) * low
        + pltpu.roll(raw, half, 1) * high
    ).astype(BF)
    grad_context = gc_ref[...]
    contexts = []
    grads = []
    for head in range(width // (3 * HEAD)):
        base = head * 3 * HEAD
        queries = turned[:, base : base + HEAD]
        keys = turned[:, base + HEAD : base + 2 * HEAD]
        values = turned[:, base + 2 * HEAD : base + 3 * HEAD]
        gc_head = grad_context[:, head * HEAD : (head + 1) * HEAD]
        dk_ref[...] = jnp.zeros_like(dk_ref)
        dv_ref[...] = jnp.zeros_like(dv_ref)
        ctx_parts = []
        dq_parts = []
        for block in range(LEN // QB):
            start, end = block * QB, (block + 1) * QB
            q, gc = queries[start:end], gc_head[start:end]
            k, v = keys[:end], values[:end]
            scores = dot(q, k, ((1,), (1,))) * SCALE
            row = lax.broadcasted_iota(jnp.int32, scores.shape, 0) + start
            col = lax.broadcasted_iota(jnp.int32, scores.shape, 1)
            masked = jnp.where(row >= col, scores, -1e30)
            top = jnp.max(masked, axis=-1, keepdims=True)
            powers = jnp.exp(masked - top)
            exact = powers * (1.0 / jnp.sum(powers, axis=-1, keepdims=True))
            probs = exact.astype(BF)
            ctx_parts.append(dot(probs, v))
            grad_probs = dot(gc, v, ((1,), (1,)))
            row_dot = jnp.sum(exact * grad_probs, axis=-1, keepdims=True)
            grad_scores = (exact * (grad_probs - row_dot) * SCALE).astype(BF)
            dq_parts.append(dot(grad_scores, k))
            dk_ref[:end] += dot(grad_scores, q, ((0,), (0,)))
            dv_ref[:end] += dot(probs, gc, ((0,), (0,)))
        contexts.append(jnp.concatenate(ctx_parts, axis=0))
        grads += [jnp.concatenate(dq_parts, axis=0), dk_ref[...], dv_ref[...]]
    ctx_ref[...] = jnp.concatenate(contexts, axis=1).astype(BF)
    joined = jnp.concatenate(grads, axis=1)
    out_ref[...] = (
        joined * cosine
        - pltpu.roll(joined, width - half, 1) * low
        - pltpu.roll(joined, half, 1) * high
    ).astype(BF)


def attention(projected, grad_context, tables):
    rows, width = projected.shape
    heads_width = grad_context.shape[1]
    sequences = rows // LEN
    table = pl.BlockSpec((LEN, width), lambda s: (0, 0))
    pairs = sequences * (width // (3 * HEAD))
    return pl.pallas_call(
        attention_kernel,
        grid=(sequences,),
        in_specs=[
            pl.BlockSpec((LEN, width), lambda s: (s, 0)),
            pl.BlockSpec((LEN, heads_width), lambda s: (s, 0)),
            table,
            table,
            table,
        ],
        out_specs=[
            pl.BlockSpec((LEN, heads_width), lambda s: (s, 0)),
            pl.BlockSpec((LEN, width), lambda s: (s, 0)),
        ],
        out_shape=[
            jax.ShapeDtypeStruct((rows, heads_width), BF),
            jax.ShapeDtypeStruct((rows, width), BF),
        ],
        scratch_shapes=[pltpu.VMEM((LEN, HEAD), F32), pltpu.VMEM((LEN, HEAD), F32)],
        cost_estimate=pl.CostEstimate(
            flops=pairs * 10 * LEN * LEN * HEAD * 8,
            bytes_accessed=rows * (width * 6 + heads_width * 4),
            transcendentals=pairs * LEN * LEN,
        ),
        compiler_params=pltpu.CompilerParams(vmem_limit_bytes=48 * 1024 * 1024),
        name="attention",
    )(projected, grad_context, *tables)


def solution(mesh):
    dp, tensor = mesh.shape["dp"], mesh.shape["tensor"]
    devices = dp * tensor
    line = dp // 2

    x_swap = [(i, i ^ 1) for i in range(dp)]
    y_swap = [(i, i ^ 2) for i in range(tensor)]
    core_swap = [(i, i ^ 1) for i in range(tensor)]

    def pairs(moves):
        return [(a * 2 + i, b * 2 + i) for a, b in moves for i in range(2)]

    near = pairs([(0, 1), (1, 0), (2, 3), (3, 2)])
    middle = pairs([(1, 2), (2, 1)])
    skip = pairs([(0, 2), (2, 0), (1, 3), (3, 1)])
    outward = pairs([(2, 3), (1, 0)])
    inward = pairs([(3, 2), (0, 1)])

    def xor(step):
        return pairs([(i, i ^ step) for i in range(line)])

    def over_dp(v, moves):
        return lax.ppermute(v, "dp", moves)

    def over_tensor(v, moves):
        return lax.ppermute(v, "tensor", moves)

    def line_gather(own):
        if line != 4:
            return [own] + [over_dp(own, xor(step)) for step in range(1, line)]
        far = over_dp(own, skip)
        first = over_dp(own, near)
        across = over_dp(own, middle)
        last = over_dp(far, outward)
        return [own, first, far, across + last]

    def line_reduce(parts):
        if line != 4:
            total = parts[0]
            for step in range(1, line):
                total = total + over_dp(parts[step].astype(BF), xor(step)).astype(F32)
            return total
        opposite = parts[3].astype(BF)
        relayed = over_dp(opposite, inward)
        across = over_dp(opposite, middle)
        first = over_dp(parts[1].astype(BF), near)
        far = over_dp((parts[2] + relayed.astype(F32)).astype(BF), skip)
        return (
            parts[0] + first.astype(F32) + across.astype(F32) + far.astype(F32)
        )

    def body(
        block_input,
        cotangent,
        norm_gains,
        norm_shifts,
        qkv_weight,
        qkv_bias,
        out_weight,
        up_weight,
        up_bias,
        down_weight,
    ):
        d, t = lax.axis_index("dp"), lax.axis_index("tensor")
        z, x = d // 2, d % 2
        y, core = t // 2, t % 2
        rows, width = block_input.shape
        block = width // line
        half = block // 2
        qkv_half = qkv_weight.shape[1] // 2
        up_half = up_weight.shape[1] // 2
        ctx_half = out_weight.shape[0] // 2

        def turn(v, axis):
            return jnp.concatenate(
                [
                    lax.dynamic_slice_in_dim(v, (z ^ step) * block, block, axis)
                    for step in range(line)
                ],
                axis,
            )

        def ordered(mine, other, index, axis):
            return jnp.where(
                index == 0,
                jnp.concatenate([mine, other], axis),
                jnp.concatenate([other, mine], axis),
            )

        def gather_rows(v):
            v = v[None]
            v = ordered(v, over_tensor(v, y_swap), y, 0)[None]
            v = ordered(v, over_dp(v, x_swap), x, 0)[:, :, None]
            return ordered(v, over_tensor(v, core_swap), core, 2).reshape(-1, width)

        def scatter_rows(v):
            v = v.astype(BF).reshape(2, 2, 2, rows, width)

            def pick(u, index, axis):
                return lax.dynamic_index_in_dim(u, index, axis, keepdims=False)

            got = over_tensor(pick(v, 1 - core, 2), core_swap)
            v = (pick(v, core, 2).astype(F32) + got.astype(F32)).astype(BF)
            got = over_dp(pick(v, 1 - x, 0), x_swap)
            v = (pick(v, x, 0).astype(F32) + got.astype(F32)).astype(BF)
            got = over_tensor(pick(v, 1 - y, 0), y_swap)
            return pick(v, y, 0).astype(F32) + got.astype(F32)

        own_rows = turn(block_input, 1)
        own_cot = turn(cotangent, 1)

        def half_of(v, index, axis):
            size = v.shape[axis] // 2
            return lax.dynamic_slice_in_dim(v, index * size, size, axis)

        def in_half(index):
            return jnp.concatenate(
                [half_of(qkv_weight, index, 1), half_of(up_weight, index, 1)], 1
            )

        def out_half(index):
            return jnp.concatenate(
                [half_of(out_weight, index, 0), half_of(down_weight, index, 0)], 0
            )

        in_block = ordered(in_half(x), over_dp(in_half(1 - x), x_swap), x, 0)
        out_block = ordered(out_half(x), over_dp(out_half(1 - x), x_swap), x, 1)
        all_rows = gather_rows(own_rows)
        in_full = jnp.concatenate(line_gather(in_block), 0)
        cot = gather_rows(own_cot)
        out_full = jnp.concatenate(line_gather(out_block), 1)

        own_small = jnp.concatenate(
            [
                norm_gains.reshape(-1),
                norm_shifts.reshape(-1),
                qkv_bias.reshape(-1).astype(F32),
                up_bias.reshape(-1).astype(F32),
            ]
        )
        count = own_small.shape[0]
        padded = -(-count // 128) * 128
        own_small = jnp.pad(own_small, (0, padded - count)).reshape(1, -1, 128)
        small = lax.all_to_all(
            jnp.broadcast_to(own_small, (devices,) + own_small.shape[1:]),
            ("dp", "tensor"),
            0,
            0,
        ).reshape(dp, tensor, padded)
        part = width // devices
        vectors = small[:, :, : 5 * part].reshape(devices, 5, part)
        vectors = turn(jnp.swapaxes(vectors, 0, 1).reshape(5, width), 1)
        gain_attn, gain_mlp, shift_attn, shift_mlp, shift_out = (vectors[i] for i in range(5))
        biases = lax.dynamic_index_in_dim(small, t, 1, keepdims=False)[:, 5 * part : count]
        qkv_count = qkv_bias.size

        def bias_of(v, shape):
            v = v.reshape((dp, 2, shape[0] // 2, shape[1]))
            v = lax.dynamic_index_in_dim(v, x, 1, keepdims=False)
            return jnp.swapaxes(v, 0, 1).reshape(-1)

        qkv_vector = bias_of(biases[:, :qkv_count], qkv_bias.shape)
        up_vector = bias_of(biases[:, qkv_count:], up_bias.shape)

        def unit_of(v):
            v = v.astype(F32)
            mean = jnp.mean(v, axis=-1, keepdims=True)
            centred = v - mean
            inverse = lax.rsqrt(jnp.mean(centred * centred, axis=-1, keepdims=True) + EPSILON)
            return centred * inverse, inverse

        unit, _ = unit_of(all_rows)
        normed_attn = (unit * gain_attn + shift_attn).astype(BF)
        normed_mlp = (unit * gain_mlp + shift_mlp).astype(BF)

        qkv_full, up_full = in_full[:, :qkv_half], in_full[:, qkv_half:]
        out_w, down_w = out_full[:ctx_half], out_full[ctx_half:]
        projected = dot(normed_attn, qkv_full) + qkv_vector
        pre_act = dot(normed_mlp, up_full) + up_vector
        activation = jax.nn.gelu(pre_act, approximate=False).astype(BF)
        slope = gelu_slope(pre_act)

        grad_context = dot(cot, out_w, ((1,), (1,))).astype(BF)
        context, grad_qkv = attention(projected, grad_context, rotary_tables(qkv_half))
        grad_down = dot(activation, cot, ((0,), (0,)))
        grad_out = dot(context, cot, ((0,), (0,)))
        out_grads = jnp.concatenate([grad_out, grad_down], 0)
        out_sum = line_reduce(
            [out_grads[:, i * block : (i + 1) * block] for i in range(line)]
        )

        grad_act = dot(cot, down_w, ((1,), (1,)))
        grad_pre = (grad_act * slope).astype(BF)
        grad_up = dot(normed_mlp, grad_pre, ((0,), (0,)))
        grad_qkv_weight = dot(normed_attn, grad_qkv, ((0,), (0,)))
        in_grads = jnp.concatenate([grad_qkv_weight, grad_up], 1)
        in_sum = line_reduce([in_grads[i * block : (i + 1) * block] for i in range(line)])

        branches = dot(context, out_w) + dot(activation, down_w)
        mixed = scatter_rows(branches)
        output = turn(
            (own_rows.astype(F32) + mixed + shift_out).astype(BF), 1
        )

        grad_normed_attn = dot(grad_qkv, qkv_full, ((1,), (1,)))
        grad_normed_mlp = dot(grad_pre, up_full, ((1,), (1,)))
        joint = grad_normed_attn * gain_attn + grad_normed_mlp * gain_mlp
        joint = scatter_rows(joint)
        own_unit, own_inverse = unit_of(own_rows)
        cot_rows = own_cot.astype(F32)
        first_mean = jnp.mean(joint, axis=-1, keepdims=True)
        second_mean = jnp.mean(joint * own_unit, axis=-1, keepdims=True)
        input_grad = turn(
            (cot_rows + own_inverse * (joint - first_mean - own_unit * second_mean)).astype(BF), 1
        )

        sums = turn(
            jnp.stack(
                [
                    jnp.sum(grad_normed_attn * unit, axis=0),
                    jnp.sum(grad_normed_mlp * unit, axis=0),
                    jnp.sum(grad_normed_attn, axis=0),
                    jnp.sum(grad_normed_mlp, axis=0),
                    jnp.sum(cot_rows, axis=0),
                ]
            ),
            1,
        )
        sums = jnp.swapaxes(sums.reshape(5, devices, part), 0, 1).reshape(devices, 5 * part)
        qkv_terms = jnp.sum(grad_qkv.astype(F32), axis=0).reshape(-1, dp, qkv_bias.shape[1])
        up_terms = jnp.sum(grad_pre.astype(F32), axis=0).reshape(-1, dp, up_bias.shape[1])
        terms = jnp.concatenate(
            [
                jnp.swapaxes(qkv_terms, 0, 1).reshape(dp, -1),
                jnp.swapaxes(up_terms, 0, 1).reshape(dp, -1),
            ],
            1,
        )
        aimed = (jnp.arange(tensor) == t).astype(F32)
        terms = (terms[:, None, :] * aimed[None, :, None]).reshape(devices, -1)
        sent = jnp.concatenate([sums, terms], 1)
        used = sent.shape[1]
        sent_width = -(-used // 128) * 128
        sent = jnp.pad(sent, ((0, 0), (0, sent_width - used))).reshape(devices, -1, 128)
        came = lax.all_to_all(sent, ("dp", "tensor"), 0, 0).reshape(line, 2, tensor, sent_width)
        came = jnp.sum(came, axis=(0, 2))
        norm_sums = (came[0] + came[1])[: 5 * part].reshape(5, part)
        split = 5 * part + qkv_count // 2
        qkv_bias_sum = came[:, 5 * part : split].reshape(qkv_bias.shape)
        up_bias_sum = came[:, split:used].reshape(up_bias.shape)

        in_mine = lax.dynamic_slice_in_dim(in_sum, x * half, half, 0)
        in_other = over_dp(
            lax.dynamic_slice_in_dim(in_sum, (1 - x) * half, half, 0).astype(BF), x_swap
        ).astype(F32)
        grad_qkv_shard = ordered(in_mine[:, :qkv_half], in_other[:, :qkv_half], x, 1)
        grad_up_shard = ordered(in_mine[:, qkv_half:], in_other[:, qkv_half:], x, 1)
        out_mine = lax.dynamic_slice_in_dim(out_sum, x * half, half, 1)
        out_other = over_dp(
            lax.dynamic_slice_in_dim(out_sum, (1 - x) * half, half, 1).astype(BF), x_swap
        ).astype(F32)
        grad_out_shard = ordered(out_mine[:ctx_half], out_other[:ctx_half], x, 0)
        grad_down_shard = ordered(out_mine[ctx_half:], out_other[ctx_half:], x, 0)
        return (
            output,
            input_grad,
            norm_sums[:2],
            norm_sums[2:],
            grad_qkv_shard,
            qkv_bias_sum,
            grad_out_shard,
            grad_up_shard,
            up_bias_sum,
            grad_down_shard,
        )

    specs = (
        P(("dp", "tensor"), None),
        P(("dp", "tensor"), None),
        P(None, ("dp", "tensor")),
        P(None, ("dp", "tensor")),
        P("dp", "tensor"),
        P("tensor", "dp"),
        P("tensor", "dp"),
        P("dp", "tensor"),
        P("tensor", "dp"),
        P("tensor", "dp"),
    )
    return jax.shard_map(body, mesh=mesh, in_specs=specs, out_specs=specs, check_vma=False)
```
